256 devices in a mesh: grp: 4 (over y), seq: 16 (over z, core), head: 4 (over x).
Axes of the slice: x: 4, y: 4, z: 8, core: 2. Of those that a mesh axis runs over, the one named last changes fastest.
Arguments:
- keys: bfloat16 [32, 8192, 1536], P('grp', 'seq', 'head'), may hold values from -6 to 6
- values: bfloat16 [32, 8192, 1536], P('grp', 'seq', 'head'), may hold values from -6 to 6
- log_forget: float32 [32, 24, 8192], P('grp', 'head', 'seq'), may hold values from -0.6 to 0, as said below
- keep: int32 [32, 8192], P('grp', 'seq'), may hold values from 0 to 1, as said below
- merge_weight: float32 [32, 8192], P('grp', 'seq'), may hold values from 0.1 to 10
- lengths: int32 [32], P('grp'), may hold values from 64 to 8192, as said below
- route: int32 [32], P('grp'), may hold values from 0 to 31, as said below
- fresh: bfloat16 [3, 32, 1536], P(None, 'grp', 'head'), may hold values from -7.5 to 7.5
- new_forget: bfloat16 [32, 24], P('grp', 'head'), may hold values from -1 to -0.049804688
- out_weight: bfloat16 [1536, 1536], P('head', 'seq'), may hold values from -0.15625 to 0.15625
Outputs:
- compact_keys: bfloat16 [32, 4096, 1536], P('grp', 'seq', 'head')
- compact_values: bfloat16 [32, 4096, 1536], P('grp', 'seq', 'head')
- compact_decay: float32 [32, 24, 4096], P('grp', 'head', 'seq')
- layer_out: bfloat16 [32, 1536], P('grp', 'seq')
The draws below stay inside these ranges and needn't reach their ends.
Inputs may be any that keep to these rules, and one draw needn't show every extreme that they name: `keep`: within every aligned block of 64 positions of a request, between 16 and 31 entries are 1, and some block has exactly 31. `lengths`: multiples of 64; the first request of every 8 in order has 8192. `route`: A permutation of the requests. `log_forget`: Negative.
All inputs are finite; a program needn't handle non-finite values.
Results may differ from the reference program's by a relative error of at most 0.0085.
Values may be sent and summed in bfloat16 or wider, within the bound.
A program may use at most 64 MiB of HBM per device.

```python
import math
import jax
import jax.numpy as jnp
from jax import lax

D = 1536
HEAD_COUNT = 24
HD = 64
BLOCK = 64
SLOTS = 32
R_GRP = 8
CACHE_LENGTH = 8192
REQUEST_COUNT = 32
NBLK = 128
ROWS = 4096
CROWS = 256
PIECE = 16
N_SEQ = 16


def pattern_parts(key):
    baseline_level = jax.random.fold_in(key, 31)
    key_head = jax.random.fold_in(baseline_level, 1)
    chosen_head = jax.random.randint(key_head, (REQUEST_COUNT,), 0, HEAD_COUNT)
    aligned = jnp.arange(REQUEST_COUNT) % 3 == 0
    return (chosen_head, aligned)


def route_common(key):
    return jax.random.permutation(jax.random.fold_in(key, 11), REQUEST_COUNT).astype(jnp.int32)


def draw_route(key, part):
    return route_common(key)


def draw_lengths(key, part):
    blocks = jax.random.randint(jax.random.fold_in(key, 5), (REQUEST_COUNT,), 1, NBLK + 1)
    full = jnp.arange(REQUEST_COUNT) % R_GRP == 0
    blocks = jnp.where(full, NBLK, blocks)
    return (blocks * BLOCK).astype(jnp.int32)


def draw_keep(key, part):
    key_count, key_order = jax.random.split(jax.random.fold_in(key, 7))
    counts = jax.random.randint(key_count, (REQUEST_COUNT, NBLK), 16, SLOTS)
    counts = counts.at[0, 0].set(SLOTS - 1)
    scores = jax.random.randint(key_order, (REQUEST_COUNT, NBLK, BLOCK), 0, 2 ** 20) * BLOCK + jnp.arange(BLOCK)[None, None, :]
    ranks = jnp.argsort(jnp.argsort(scores, axis=2), axis=2)
    flags = (ranks < counts[:, :, None]).astype(jnp.int32)
    return flags.reshape(REQUEST_COUNT, CACHE_LENGTH)


def draw_log_forget(key, part):
    baseline_level = jax.random.fold_in(key, 13)
    variety_random_key, quick_random_key, gradual_random_key, noise_random_key, spike_random_key, removal_random_key = jax.random.split(baseline_level, 6)
    chosen_head, aligned = pattern_parts(key)
    fast_share = 0.5
    fast = jax.random.uniform(variety_random_key, (REQUEST_COUNT, HEAD_COUNT)) < fast_share
    forced = aligned[:, None] & (jnp.arange(HEAD_COUNT)[None, :] == chosen_head[:, None])
    fast = fast & jnp.logical_not(forced)
    fast_rate = jnp.exp(jax.random.uniform(quick_random_key, (REQUEST_COUNT, HEAD_COUNT), jnp.float32, math.log(1.0 / 50.0), math.log(1.0 / 30.0)))
    slow_rate = jnp.exp(jax.random.uniform(gradual_random_key, (REQUEST_COUNT, HEAD_COUNT), jnp.float32, math.log(0.1), math.log(0.8))) / CACHE_LENGTH
    decay_speed = jnp.where(fast, fast_rate, slow_rate)
    noisy_part = jnp.exp(jax.random.uniform(noise_random_key, (REQUEST_COUNT, HEAD_COUNT, CACHE_LENGTH), jnp.float32, math.log(0.5), math.log(2.0)))
    sudden_spike = jax.random.uniform(spike_random_key, (REQUEST_COUNT, HEAD_COUNT, CACHE_LENGTH)) < 2.0 / CACHE_LENGTH
    removal_flags = jax.random.uniform(removal_random_key, (REQUEST_COUNT, HEAD_COUNT, CACHE_LENGTH), jnp.float32, math.log(0.6), math.log(0.85))
    return -decay_speed[:, :, None] * noisy_part + jnp.where(sudden_spike, removal_flags, 0.0)


def draw_keys(key, part):
    base_key = jax.random.fold_in(key, 17)
    key_base = jax.random.fold_in(base_key, 0)
    baseline_level = jnp.clip(jax.random.normal(key_base, (REQUEST_COUNT, CACHE_LENGTH, D), jnp.float32), -6.0, 6.0)
    return baseline_level.astype(jnp.bfloat16)


def draw_fresh(key, part):
    key_base = jax.random.fold_in(key, 19)
    baseline_level = jnp.clip(jax.random.normal(key_base, (3, REQUEST_COUNT, D), jnp.float32), -6.0, 6.0)
    return baseline_level.astype(jnp.bfloat16)


def steps_of(key, shape, pieces, smallest, largest):
    level, own = 1.0, jax.random.fold_in(key, 6)
    for dim, shards_of in pieces:
        draws = jnp.exp(jax.random.uniform(jax.random.fold_in(own, dim), (shards_of,), jnp.float32, smallest / len(pieces), largest / len(pieces)))
        level = level * jnp.repeat(draws, shape[dim] // shards_of).reshape([-1 if axis == dim else 1 for axis in range(len(shape))])
    return level


def normal_values(key, dims, width, most, pieces=(), held_as=jnp.bfloat16):
    entries = jax.random.normal(key, dims, jnp.float32) * width
    if len(pieces) > 0:
        entries = steps_of(key, dims, pieces, -0.22, 0.18) * entries
    return jnp.clip(entries, min=-most, max=most).astype(held_as)


def setup_inputs(seed: int = 0) -> dict:
    streams_of = jax.random.split(jax.random.key(seed), 11)
    keys = draw_keys(jax.random.fold_in(streams_of[10], 71), 0)
    values = normal_values(streams_of[1], (REQUEST_COUNT, CACHE_LENGTH, D), 1.0, 6.0, ((0, 4), (1, 16), (2, 4)))
    log_forget = draw_log_forget(jax.random.fold_in(streams_of[10], 71), 0)
    keep = draw_keep(jax.random.fold_in(streams_of[10], 71), 0)
    merge_weight = jnp.clip(jnp.exp(math.log(10.0) - 4.6051702 * jax.random.uniform(streams_of[4], (REQUEST_COUNT, CACHE_LENGTH), jnp.float32) ** steps_of(streams_of[4], (REQUEST_COUNT, CACHE_LENGTH), ((0, 4), (1, 16)), -0.2, 0.2)), 0.1, 10.0)
    lengths = draw_lengths(jax.random.fold_in(streams_of[10], 71), 0)
    route = draw_route(jax.random.fold_in(streams_of[10], 71), 0)
    fresh = draw_fresh(jax.random.fold_in(streams_of[10], 71), 0)
    new_forget = jnp.clip(-1.0 + 0.9501953 * jax.random.uniform(streams_of[8], (REQUEST_COUNT, HEAD_COUNT), jnp.float32) ** steps_of(streams_of[8], (REQUEST_COUNT, HEAD_COUNT), ((0, 4), (1, 4)), -0.2, 0.2), -1.0, -0.049804688).astype(jnp.bfloat16)
    out_weight = normal_values(streams_of[9], (D, D), D ** -0.5, 0.15625, ((0, 4), (1, 16)))
    return {"keys": keys, "values": values, "log_forget": log_forget, "keep": keep, "merge_weight": merge_weight, "lengths": lengths, "route": route, "fresh": fresh, "new_forget": new_forget, "out_weight": out_weight}


EMPTY_LOG = -1.0e4


def reference(keys, values, log_forget, keep, merge_weight, lengths, route, fresh, new_forget, out_weight):
    scale = HD ** -0.5

    def one_request(index):
        length = lengths[index]
        position = jnp.arange(CACHE_LENGTH, dtype=jnp.int32)
        live = position < length
        forget = jnp.where(live[None, :], log_forget[index], 0.0)
        log_decay = jnp.sum(forget, axis=1, keepdims=True) - jnp.cumsum(forget, axis=1)
        flags = keep[index].reshape(NBLK, BLOCK)
        rank = jnp.cumsum(flags, axis=1) - 1
        slot_ids = jnp.arange(SLOTS - 1, dtype=jnp.int32)
        block_live = (jnp.arange(NBLK, dtype=jnp.int32) * BLOCK < length).astype(jnp.float32)
        chosen = ((flags[:, None, :] == 1) & (rank[:, None, :] == slot_ids[None, :, None])).astype(jnp.float32)
        chosen = chosen * block_live[:, None, None]
        dropped = flags == 0
        weighted = jnp.where(dropped, merge_weight[index].reshape(NBLK, BLOCK), 0.0)
        share = (weighted / jnp.sum(weighted, axis=1, keepdims=True)).astype(jnp.bfloat16).astype(jnp.float32)
        select = jnp.concatenate([chosen, (share * block_live[:, None])[:, None, :]], axis=1)
        key_blocks = keys[index].reshape(NBLK, BLOCK, D).astype(jnp.float32)
        value_blocks = values[index].reshape(NBLK, BLOCK, D).astype(jnp.float32)
        packed_keys = jnp.einsum("bej,bjc->bec", select, key_blocks, precision=lax.Precision.HIGHEST).astype(jnp.bfloat16).reshape(ROWS, D)
        packed_values = jnp.einsum("bej,bjc->bec", select, value_blocks, precision=lax.Precision.HIGHEST).astype(jnp.bfloat16).reshape(ROWS, D)
        decay_blocks = log_decay.reshape(HEAD_COUNT, NBLK, BLOCK)
        kept_log = jnp.einsum("bej,hbj->hbe", chosen, decay_blocks, precision=lax.Precision.HIGHEST)
        filled = jnp.sum(chosen, axis=2)
        kept_log = kept_log + (1.0 - filled)[None, :, :] * EMPTY_LOG
        drop_mask = dropped[None, :, :]
        drop_peak = jnp.max(jnp.where(drop_mask, decay_blocks, -jnp.inf), axis=2)
        spread = jnp.where(drop_mask, jnp.exp(decay_blocks - drop_peak[:, :, None]), 0.0)
        merged_log = drop_peak + jnp.log(jnp.sum(share[None, :, :] * spread, axis=2))
        merged_log = jnp.where(block_live[None, :] > 0, merged_log, EMPTY_LOG)
        slot_log = jnp.concatenate([kept_log, merged_log[:, :, None]], axis=2).reshape(HEAD_COUNT, ROWS)
        arrival = route[index]
        query = fresh[0, arrival].reshape(HEAD_COUNT, HD).astype(jnp.float32)
        own_key = fresh[1, arrival].reshape(HEAD_COUNT, HD).astype(jnp.float32)
        own_value = fresh[2, arrival].reshape(HEAD_COUNT, HD).astype(jnp.float32)
        new_log = new_forget[arrival].astype(jnp.float32)
        key_rows = packed_keys.reshape(ROWS, HEAD_COUNT, HD).astype(jnp.float32)
        value_rows = packed_values.reshape(N_SEQ, CROWS, HEAD_COUNT, HD).astype(jnp.float32)
        scores = jnp.einsum("hd,nhd->hn", query, key_rows, precision=lax.Precision.HIGHEST) * scale + slot_log
        runs = scores.reshape(HEAD_COUNT, N_SEQ, CROWS)
        run_top = jnp.max(runs, axis=2)
        weights = jnp.exp(runs - run_top[:, :, None]).astype(jnp.bfloat16).astype(jnp.float32)
        run_sum = jnp.sum(weights, axis=2)
        run_acc = jnp.einsum("hsn,snhd->hsd", weights, value_rows, precision=lax.Precision.HIGHEST)
        top = jnp.max(run_top, axis=1)
        rescale = jnp.exp(run_top - top[:, None])
        total_sum = jnp.sum(rescale * run_sum, axis=1)
        total_acc = jnp.sum(rescale[:, :, None] * run_acc, axis=1)
        own_score = jnp.sum(query * own_key, axis=1) * scale
        cache_top = top + new_log
        joint = jnp.maximum(cache_top, own_score)
        cache_scale = jnp.exp(cache_top - joint)
        self_weight = jnp.exp(own_score - joint)
        attended = (cache_scale[:, None] * total_acc + self_weight[:, None] * own_value) / (cache_scale * total_sum + self_weight)[:, None]
        attended = attended.reshape(D).astype(jnp.bfloat16)
        dealt_keys = packed_keys.reshape(N_SEQ, N_SEQ, PIECE, D).transpose(1, 0, 2, 3).reshape(ROWS, D)
        dealt_values = packed_values.reshape(N_SEQ, N_SEQ, PIECE, D).transpose(1, 0, 2, 3).reshape(ROWS, D)
        return dealt_keys, dealt_values, jnp.exp(slot_log), attended

    compact_keys, compact_values, compact_decay, attended = lax.map(one_request, jnp.arange(REQUEST_COUNT, dtype=jnp.int32))
    layer_out = jnp.dot(attended, out_weight, preferred_element_type=jnp.float32).astype(jnp.bfloat16)
    return compact_keys, compact_values, compact_decay, layer_out
```

```python
import jax
import jax.numpy as jnp
from jax import lax
from jax.sharding import PartitionSpec as P

BLOCK = 64
SLOTS = 32


EMPTY_LOG = -10000.0
HIGHEST = lax.Precision.HIGHEST


def shards(
    keys, values, log_forget, keep, merge_weight, lengths, route, fresh, new_forget, out_weight
):
    f32, bf16 = jnp.float32, jnp.bfloat16
    req_dev, pos_dev, width_dev = keys.shape
    heads_dev = log_forget.shape[1]
    head_size = width_dev // heads_dev
    blocks_dev = pos_dev // BLOCK
    rows_dev = blocks_dev * SLOTS
    n_seq = lax.axis_size("seq")
    shard = lax.axis_index("seq")

    grp_req = fresh.shape[1]
    packed_fresh = jnp.concatenate(
        [fresh.transpose(1, 0, 2).reshape(grp_req, 3 * width_dev), new_forget], axis=1
    )
    arrived = lax.all_gather(packed_fresh, "grp", axis=0, tiled=True)
    picked = jnp.take(arrived, route, axis=0)
    query = picked[:, :width_dev]
    own_key = picked[:, width_dev : 2 * width_dev]
    own_value = picked[:, 2 * width_dev : 3 * width_dev].astype(f32)
    new_log = picked[:, 3 * width_dev :].astype(f32)

    position = shard * pos_dev + jnp.arange(pos_dev, dtype=jnp.int32)
    live = position[None, :] < lengths[:, None]
    forget = jnp.where(live[:, None, :], log_forget, 0.0)
    forget_blocks = forget.reshape(req_dev, heads_dev, blocks_dev, BLOCK)
    at = jnp.arange(BLOCK, dtype=jnp.int32)
    after = (at[:, None] > at[None, :]).astype(f32)
    within = jnp.einsum("rhbt,tp->rhbp", forget_blocks, after, precision=HIGHEST)
    block_total = jnp.sum(forget_blocks, axis=3)
    own_total = jnp.sum(block_total, axis=2)
    bt = jnp.arange(blocks_dev, dtype=jnp.int32)
    later_block = jnp.einsum(
        "rhb,bc->rhc", block_total, (bt[:, None] > bt[None, :]).astype(f32), precision=HIGHEST
    )
    totals = lax.all_gather(own_total, "seq")
    later_shard = jnp.sum(
        jnp.where((jnp.arange(n_seq) > shard)[:, None, None], totals, 0.0), axis=0
    )
    decay_blocks = within + later_block[..., None] + later_shard[:, :, None, None]

    flags = keep.reshape(req_dev, blocks_dev, BLOCK)
    upto = (at[:, None] <= at[None, :]).astype(bf16)
    rank = (
        jnp.einsum("rbt,tp->rbp", flags.astype(bf16), upto, preferred_element_type=f32).astype(
            jnp.int32
        )
        - 1
    )
    slot_ids = jnp.arange(SLOTS - 1, dtype=jnp.int32)
    block_start = shard * pos_dev + bt * BLOCK
    block_live = (block_start[None, :] < lengths[:, None]).astype(f32)
    chosen = (
        (flags[:, :, None, :] == 1) & (rank[:, :, None, :] == slot_ids[None, None, :, None])
    ).astype(f32)
    chosen = chosen * block_live[:, :, None, None]
    dropped = flags == 0
    weighted = jnp.where(dropped, merge_weight.reshape(req_dev, blocks_dev, BLOCK), 0.0)
    share = (
        (weighted / jnp.sum(weighted, axis=2, keepdims=True)).astype(bf16).astype(f32)
    )
    merged_row = (share * block_live[:, :, None])[:, :, None, :]
    select = jnp.concatenate([chosen, merged_row], axis=2).astype(bf16)
    key_blocks = keys.reshape(req_dev, blocks_dev, BLOCK, width_dev)
    value_blocks = values.reshape(req_dev, blocks_dev, BLOCK, width_dev)
    packed_keys = (
        jnp.einsum("rbej,rbjc->rbec", select, key_blocks, preferred_element_type=f32)
        .astype(bf16)
        .reshape(req_dev, rows_dev, width_dev)
    )
    packed_values = (
        jnp.einsum("rbej,rbjc->rbec", select, value_blocks, preferred_element_type=f32)
        .astype(bf16)
        .reshape(req_dev, rows_dev, width_dev)
    )
    dealt = lax.all_to_all(
        jnp.stack([packed_keys, packed_values]), "seq", split_axis=2, concat_axis=2, tiled=True
    )

    kept_log = jnp.einsum("rbej,rhbj->rhbe", chosen, decay_blocks, precision=HIGHEST)
    filled = jnp.sum(chosen, axis=3)
    kept_log = kept_log + (1.0 - filled)[:, None, :, :] * EMPTY_LOG
    drop_mask = dropped[:, None, :, :]
    drop_peak = jnp.max(jnp.where(drop_mask, decay_blocks, -jnp.inf), axis=3)
    spread = jnp.where(drop_mask, jnp.exp(decay_blocks - drop_peak[..., None]), 0.0)
    merged_log = drop_peak + jnp.log(jnp.sum(share[:, None, :, :] * spread, axis=3))
    merged_log = jnp.where(block_live[:, None, :] > 0, merged_log, EMPTY_LOG)
    slot_log = jnp.concatenate([kept_log, merged_log[..., None]], axis=3).reshape(
        req_dev, heads_dev, rows_dev
    )
    compact_decay = jnp.exp(slot_log)

    scale = head_size ** (-0.5)
    head_of = jnp.arange(width_dev, dtype=jnp.int32) // head_size
    onehot = head_of[:, None] == jnp.arange(heads_dev, dtype=jnp.int32)[None, :]
    query_blocks = jnp.where(onehot[None], query[:, :, None], jnp.zeros((), bf16))
    scores = (
        jnp.einsum("rnc,rch->rhn", packed_keys, query_blocks, preferred_element_type=f32) * scale
        + slot_log
    )
    local_top = jnp.max(scores, axis=2)
    weights = jnp.exp(scores - local_top[..., None]).astype(bf16)
    local_sum = jnp.sum(weights.astype(f32), axis=2)
    full_acc = jnp.einsum("rhn,rnc->rhc", weights, packed_values, preferred_element_type=f32)
    local_acc = jnp.sum(jnp.where(onehot.T[None], full_acc, 0.0), axis=1)
    stats = jnp.concatenate([local_top, local_sum, local_acc], axis=1)
    every = lax.all_gather(stats, "seq")
    tops = every[:, :, :heads_dev]
    sums = every[:, :, heads_dev : 2 * heads_dev]
    accs = every[:, :, 2 * heads_dev :]
    top = jnp.max(tops, axis=0)
    rescale = jnp.exp(tops - top[None])
    total_sum = jnp.sum(rescale * sums, axis=0)
    total_acc = jnp.sum(jnp.repeat(rescale, head_size, axis=2) * accs, axis=0)

    own_score = (
        jnp.sum(
            (query.astype(f32) * own_key.astype(f32)).reshape(req_dev, heads_dev, head_size),
            axis=2,
        )
        * scale
    )
    cache_top = top + new_log
    joint = jnp.maximum(cache_top, own_score)
    cache_scale = jnp.exp(cache_top - joint)
    self_weight = jnp.exp(own_score - joint)
    numer = (
        jnp.repeat(cache_scale, head_size, axis=1) * total_acc
        + jnp.repeat(self_weight, head_size, axis=1) * own_value
    )
    denom = jnp.repeat(cache_scale * total_sum + self_weight, head_size, axis=1)
    attended = (numer / denom).astype(bf16)
    partial_out = jnp.dot(attended, out_weight, preferred_element_type=f32)
    layer_out = lax.psum(partial_out, "head").astype(bf16)
    return (dealt[0], dealt[1], compact_decay, layer_out)


def solution(mesh):
    return jax.shard_map(
        shards,
        mesh=mesh,
        in_specs=(
            P("grp", "seq", "head"),
            P("grp", "seq", "head"),
            P("grp", "head", "seq"),
            P("grp", "seq"),
            P("grp", "seq"),
            P("grp"),
            P("grp"),
            P(None, "grp", "head"),
            P("grp", "head"),
            P("head", "seq"),
        ),
        out_specs=(
            P("grp", "seq", "head"),
            P("grp", "seq", "head"),
            P("grp", "head", "seq"),
            P("grp", "seq"),
        ),
        check_vma=False,
    )
```
